32 devices in a mesh: depth: 4 (over y, x), chan: 8 (over z, core).
Axes of the slice: x: 2, y: 2, z: 4, core: 2. Of those that a mesh axis runs over, the one named last changes fastest.
Arguments:
- volume: float32 [512, 16, 1024], P('chan', 'depth'), may hold values from -6 to 6
- conv_weight: float32 [1, 3, 16, 32, 864], P(None, None, 'chan'), may hold values from -0.21875 to 0.21875
- norm_gain: float32 [1, 512], replicated, may hold values from 0.1 to 1.9
- mlp_in: float32 [1, 1024, 512], replicated, may hold values from -0.25 to 0.25
- mlp_out: float32 [1, 512, 1024], replicated, may hold values from -0.1875 to 0.1875
Outputs:
- features: float32 [512, 16, 1024], P('chan', 'depth')
The draws below stay inside these ranges and needn't reach their ends.
All inputs are finite; a program needn't handle non-finite values.
Results may differ from the reference program's by a relative error of at most 0.0001.
Values sent between devices are 32-bit elements; how exact they have to be, the bound alone decides.
A program may use at most 64 MiB of HBM per device.

```python
import jax
import jax.numpy as jnp
from jax import lax

C = 512
CG = 32
HID = 1024
H = 32
W = 32
BLOCKS = 1
CONVS = 3
GROUPS = 16
TAPS = 864
NZ = 16
HW = 1024


def block_scale(rng, dims, shards, least, top_value):
    gain = 1.0
    for position, parts in shards:
        draws = jax.random.uniform(jax.random.fold_in(jax.random.fold_in(rng, 6), position), (parts,), jnp.float32, least / len(shards), top_value / len(shards))
        gain = gain * jnp.repeat(jnp.exp(draws), dims[position] // parts).reshape((-1,) + (1,) * (len(dims) - 1 - position))
    return gain


def normal_values(rng, shape, deviation, bound, pieces=(), held_as=jnp.bfloat16):
    entries = deviation * jax.random.normal(rng, shape, jnp.float32)
    if pieces:
        entries = entries * block_scale(rng, shape, pieces, -0.22, 0.18)
    return jnp.clip(entries, -bound, bound).astype(held_as)


def setup_inputs(seed: int = 0) -> dict:
    keys = jax.random.split(jax.random.key(seed), 6)
    return {
        "volume": normal_values(keys[0], (C, NZ, HW), 1.0, 6.0, ((0, 8), (1, 4)), jnp.float32),
        "conv_weight": normal_values(keys[1], (BLOCKS, CONVS, GROUPS, CG, TAPS), TAPS ** -0.5, 0.21875, ((2, 8),), jnp.float32),
        "norm_gain": jnp.clip(1.0 + 0.18 * jax.random.normal(keys[2], (BLOCKS, C), jnp.float32), 0.1, 1.9),
        "mlp_in": normal_values(keys[3], (BLOCKS, HID, C), C ** -0.5, 0.25, (), jnp.float32),
        "mlp_out": normal_values(keys[4], (BLOCKS, C, HID), HID ** -0.5, 0.1875, (), jnp.float32),
    }


def convolve(field, kernel):
    grouped = field.reshape(GROUPS, CG, NZ, H, W)
    total = jnp.zeros_like(grouped)
    for shift_h in range(3):
        for shift_w in range(3):
            for shift_d in range(3):
                moved = jnp.roll(grouped, (1 - shift_d, 1 - shift_h, 1 - shift_w), (2, 3, 4))
                start = ((shift_h * 3 + shift_w) * 3 + shift_d) * CG
                piece = kernel[:, :, start:start + CG]
                total = total + jnp.einsum('goi,gizhw->gozhw', piece, moved, precision=lax.Precision.HIGHEST)
    return total.reshape(C, NZ, H * W)

def reference(volume, conv_weight, norm_gain, mlp_in, mlp_out):
    state = volume
    for block in range(BLOCKS):
        inner = jax.nn.gelu(convolve(state, conv_weight[block, 0]))
        inner = jax.nn.gelu(convolve(inner, conv_weight[block, 1]))
        mixed = state + convolve(inner, conv_weight[block, 2])
        flat = mixed.reshape(C, -1)
        scaled = flat * lax.rsqrt(lax.optimization_barrier(jnp.mean(flat * flat, axis=0)) + 1e-06) * norm_gain[block][:, None]
        hidden = jax.nn.gelu(jnp.dot(mlp_in[block], scaled, precision=lax.Precision.HIGHEST))
        flat = flat + jnp.dot(mlp_out[block], hidden, precision=lax.Precision.HIGHEST)
        state = flat.reshape(C, NZ, H * W)
    return state
```

```python
import functools

import jax
import jax.numpy as jnp
from jax import lax
from jax.experimental import pallas as pl
from jax.experimental.pallas import tpu as pltpu
from jax.sharding import PartitionSpec as P

W = 32
LANES = 128
LIMIT = 60 * 1024 * 1024
MESH = pl.DeviceIdType.MESH


def split(x):
    hi = x.astype(jnp.bfloat16)
    return hi, (x - hi.astype(jnp.float32)).astype(jnp.bfloat16)


def dot(a, b):
    return jnp.dot(a, b, preferred_element_type=jnp.float32)


def block_body(
    depth, chan, vin, wconv, gain, w_in, w_out, out,
    xs, xb, acc, wraw, wf, wmat, edge, halo, ybuf, rin, obuf,
    in_f, out_f, in_hi, in_lo, out_hi, out_lo, r_hi, r_lo, mo,
    x_recv, w_sem, halo_send, swap_send, edge_send, edge_recv,
    y_send, y_recv, o_send, o_recv,
):
    groups, planes, width, cells = vin.shape
    total = groups * planes
    teams = depth // groups
    tiles = cells // LANES
    rows = chan // tiles
    slots = planes // rows
    channels = groups * width
    part = 3 * width
    span = 3 * part

    d = lax.axis_index("depth")
    c = lax.axis_index("chan")
    j = lax.rem(d, groups)
    t = lax.div(d, groups)
    tile = lax.rem(c, tiles)
    row = lax.div(c, tiles)
    flip = j > 0
    above = lax.rem(t + 1, teams)
    below = lax.rem(t + teams - 1, teams)

    def place(q):
        return jnp.where(flip, total - 1 - q, q)

    barrier = pltpu.get_barrier_semaphore()
    peers = 0
    for team in (above, below) if teams > 2 else (above,):
        for k in range(groups):
            pl.semaphore_signal(barrier, inc=1, device_id={"depth": team * groups + k}, device_id_type=MESH)
            peers += 1
    for g in range(groups):
        for k in range(1 if g == 0 else 0, chan):
            pl.semaphore_signal(
                barrier, inc=1,
                device_id={"depth": t * groups + lax.rem(j + g, groups), "chan": lax.rem(c + k, chan)},
                device_id_type=MESH,
            )
            peers += 1

    loads = [pltpu.make_async_copy(wconv.at[0, l, j], wraw.at[l], w_sem.at[l]) for l in range(3)]
    for load in loads:
        load.start()
    for z in range(planes):
        slot = j * planes + z + 1
        pltpu.make_async_copy(vin.at[j, z], xs.at[slot], x_recv.at[slot]).start()
    in_load = pltpu.make_async_copy(w_in.at[0], in_f, w_sem.at[3])
    out_load = pltpu.make_async_copy(w_out.at[0], out_f, w_sem.at[4])
    in_load.start()
    out_load.start()

    pl.semaphore_wait(barrier, peers)

    def halo_copy(side, k):
        return pltpu.make_async_remote_copy(
            src_ref=vin.at[k, 0 if side == 0 else planes - 1],
            dst_ref=xs.at[total + 1 if side == 0 else 0],
            send_sem=halo_send.at[side, k],
            recv_sem=x_recv.at[total + 1 if side == 0 else 0],
            device_id={"depth": (below if side == 0 else above) * groups + k},
            device_id_type=MESH,
        )

    def swap_copy(k, i):
        peer = lax.rem(j + k, groups)
        z = jnp.where(peer == 0, i, planes - 1 - i)
        slot = j * planes + z + 1
        return pltpu.make_async_remote_copy(
            src_ref=vin.at[peer, z],
            dst_ref=xs.at[slot],
            send_sem=swap_send.at[k, i],
            recv_sem=x_recv.at[slot],
            device_id={"depth": t * groups + peer},
            device_id_type=MESH,
        )

    @pl.when(j == 0)
    def _():
        for k in reversed(range(groups)):
            halo_copy(0, k).start()

    @pl.when(j == groups - 1)
    def _():
        for k in range(groups):
            halo_copy(1, k).start()

    for i in range(planes):
        for k in range(1, groups):
            swap_copy(k, i).start()

    for l in range(3):
        loads[l].wait()
        for b in range(3):
            for e in range(3):
                for a in range(3):
                    start = ((b * 3 + e) * 3 + a) * width
                    piece = wraw[l, :, start : start + width]
                    hi = piece.astype(jnp.bfloat16).astype(jnp.float32)
                    for n, value in enumerate((hi, hi, piece - hi)):
                        col = ((a * 3 + n) * 3 + e) * width
                        wf[b * width : (b + 1) * width, col : col + width] = value
        wmat[l] = wf[...].astype(jnp.bfloat16)

    in_load.wait()
    out_load.wait()
    hidden = in_f.shape[0]
    step = 64

    def widen(k, _):
        at = pl.ds(pl.multiple_of(k * step, step), step)
        in_hi[at, :], in_lo[at, :] = split(in_f[at, :] * gain[...])
        return 0

    lax.fori_loop(0, hidden // step, widen, 0)

    def widen(k, _):
        at = pl.ds(pl.multiple_of(k * step, step), step)
        out_hi[at, :], out_lo[at, :] = split(out_f[at, :])
        return 0

    lax.fori_loop(0, out_f.shape[0] // step, widen, 0)

    column = lax.broadcasted_iota(jnp.int32, (width, cells), 1) % W

    def prepare(l, slot, x):
        before = jnp.where(column == 0, pltpu.roll(x, cells + 1 - W, 1), pltpu.roll(x, 1, 1))
        after = jnp.where(column == W - 1, pltpu.roll(x, W - 1, 1), pltpu.roll(x, cells - 1, 1))
        for e, value in enumerate((before, x, after)):
            hi, lo = split(value)
            for n, piece in enumerate((hi, lo, hi)):
                at = pl.multiple_of(slot * span + (n * 3 + e) * width, width)
                xb[l, pl.ds(at, width), :] = piece

    def conv(l, p):
        at = pl.ds(pl.multiple_of(p * span, width), 3 * span)
        for n in range(0, cells, 256):
            acc[:, n : n + 256] = dot(wmat[l], xb[l, at, n : n + 256])
        p0, p1, p2 = (acc[b * width : (b + 1) * width, :] for b in range(3))
        return p1 + pltpu.roll(p0, W, 1) + pltpu.roll(p2, cells - W, 1)

    def arrive(q):
        slot = place(q) + 1
        pltpu.make_async_copy(xs.at[slot], xs.at[slot], x_recv.at[slot]).wait()
        prepare(0, slot, xs[slot])

    def edge_copy(l, side):
        front = jnp.where(flip, above, below)
        back = jnp.where(flip, below, above)
        return pltpu.make_async_remote_copy(
            src_ref=edge.at[l, side],
            dst_ref=halo.at[l, 1 - side],
            send_sem=edge_send.at[l, side],
            recv_sem=edge_recv.at[l, 1 - side],
            device_id={"depth": (front if side == 0 else back) * groups + j},
            device_id_type=MESH,
        )

    def send_edge(l, side, u):
        edge[l, side] = u
        edge_copy(l, side).start()

    def take_halo(l, side):
        pltpu.make_async_copy(halo.at[l, side], halo.at[l, side], edge_recv.at[l, side]).wait()
        prepare(l + 1, place(-1 if side == 0 else total) + 1, halo[l, side])

    def inner(l, q):
        p = place(q)
        u = jax.nn.gelu(conv(l, p))
        prepare(l + 1, p + 1, u)
        return u

    def y_target(p, k):
        z = lax.rem(p, planes)
        m = lax.div(p, planes)
        at = lax.rem(tile + tiles // 2 + k, tiles)
        peer = lax.rem(z, rows) * tiles + at
        own = jnp.logical_and(m == j, peer == c)
        src = ybuf.at[p, :, pl.ds(pl.multiple_of(at * LANES, LANES), LANES)]
        slot = lax.div(z, rows)
        first = pl.multiple_of((c * groups + j) * width, width)
        dst = rin.at[slot, pl.ds(first, width), :]
        copy = pltpu.make_async_remote_copy(
            src_ref=src, dst_ref=dst, send_sem=y_send.at[p, k], recv_sem=y_recv.at[slot],
            device_id={"depth": t * groups + m, "chan": peer}, device_id_type=MESH,
        )
        return own, copy, src, dst, y_recv.at[slot]

    def outer(q):
        p = place(q)
        ybuf[p] = xs[p + 1] + conv(2, p)

        def send(k, _):
            own, copy, src, dst, sem = y_target(p, k)

            @pl.when(own)
            def _():
                pltpu.make_async_copy(src, dst, sem).start()

            @pl.when(jnp.logical_not(own))
            def _():
                copy.start()

            return 0

        lax.fori_loop(0, tiles, send, 0)

    arrive(-1)
    arrive(0)

    def wave(i, _):
        arrive(i + 1)
        u = inner(0, i)

        @pl.when(i == 0)
        def _():
            send_edge(0, 0, u)

        @pl.when(i == total - 1)
        def _():
            send_edge(0, 1, u)

        @pl.when(i >= 2)
        def _():
            inner(1, i - 1)

        @pl.when(i >= 4)
        def _():
            outer(i - 2)

        return 0

    lax.fori_loop(0, total, wave, 0)
    take_halo(0, 1)
    send_edge(1, 1, inner(1, total - 1))
    outer(total - 2)
    take_halo(0, 0)
    send_edge(1, 0, inner(1, 0))
    outer(1)
    take_halo(1, 0)
    outer(0)
    take_halo(1, 1)
    outer(total - 1)

    block = min(256, hidden)
    chunks = slots // 2

    def o_target(slot, k):
        peer = lax.rem(c + chan // 2 + k, chan)
        first = pl.multiple_of(peer * channels, channels)
        src = obuf.at[slot, pl.ds(first, channels), :]
        dst = out.at[slot * rows + row, :, pl.ds(pl.multiple_of(tile * LANES, LANES), LANES)]
        copy = pltpu.make_async_remote_copy(
            src_ref=src, dst_ref=dst, send_sem=o_send.at[slot, k], recv_sem=o_recv,
            device_id={"chan": peer}, device_id_type=MESH,
        )
        return peer == c, copy, src, dst

    def chunk(n, _):
        first = jnp.where(flip, n, chunks - 1 - n) * 2
        for s in range(2):
            pltpu.make_async_copy(rin.at[first + s], rin.at[first + s], y_recv.at[first + s]).wait()
            x = rin[first + s]
            r = x * lax.rsqrt(jnp.mean(x * x, axis=0, keepdims=True) + 1e-06)
            at = slice(s * LANES, (s + 1) * LANES)
            r_hi[:, at], r_lo[:, at] = split(r)
            mo[:, at] = x

        def mix(k, _):
            at = pl.ds(pl.multiple_of(k * block, block), block)
            h = dot(in_hi[at, :], r_hi[...]) + (dot(in_hi[at, :], r_lo[...]) + dot(in_lo[at, :], r_hi[...]))
            h_hi, h_lo = split(jax.nn.gelu(h))
            mo[...] += dot(out_hi[:, at], h_hi) + (dot(out_hi[:, at], h_lo) + dot(out_lo[:, at], h_hi))
            return 0

        lax.fori_loop(0, hidden // block, mix, 0)
        for s in range(2):
            obuf[first + s] = mo[:, s * LANES : (s + 1) * LANES]

            def send(k, _):
                own, copy, src, dst = o_target(first + s, k)

                @pl.when(own)
                def _():
                    pltpu.make_async_copy(src, dst, o_recv).start()

                @pl.when(jnp.logical_not(own))
                def _():
                    copy.start()

                return 0

            lax.fori_loop(0, chan, send, 0)
        return 0

    lax.fori_loop(0, chunks, chunk, 0)

    @pl.when(j == 0)
    def _():
        for k in range(groups):
            halo_copy(0, k).wait_send()

    @pl.when(j == groups - 1)
    def _():
        for k in range(groups):
            halo_copy(1, k).wait_send()

    for i in range(planes):
        for k in range(1, groups):
            swap_copy(k, i).wait_send()
    for l in range(2):
        for side in range(2):
            edge_copy(l, side).wait_send()

    def drain(n, _):
        own, copy, *_ = y_target(lax.div(n, tiles), lax.rem(n, tiles))

        @pl.when(jnp.logical_not(own))
        def _():
            copy.wait_send()

        return 0

    lax.fori_loop(0, total * tiles, drain, 0)

    def drain(n, _):
        own, copy, *_ = o_target(lax.div(n, chan), lax.rem(n, chan))

        @pl.when(jnp.logical_not(own))
        def _():
            copy.wait_send()

        return 0

    lax.fori_loop(0, slots * chan, drain, 0)
    pltpu.make_async_copy(out, out, o_recv).wait()


def per_device(volume, conv_weight, norm_gain, mlp_in, mlp_out):
    channels, planes, cells = volume.shape
    width, taps = conv_weight.shape[-2:]
    groups = channels // width
    depth, chan = lax.axis_size("depth"), lax.axis_size("chan")
    total = groups * planes
    tiles = cells // LANES
    slots = planes // (chan // tiles)
    hidden, every = mlp_in.shape[1:]
    vin = volume.reshape(groups, width, planes, cells).transpose(0, 2, 1, 3)
    f32, bf16 = jnp.float32, jnp.bfloat16
    dma = pltpu.SemaphoreType.DMA
    anywhere = pl.BlockSpec(memory_space=pl.ANY)
    out = pl.pallas_call(
        functools.partial(block_body, depth, chan),
        in_specs=[anywhere, anywhere, pl.BlockSpec(memory_space=pltpu.VMEM), anywhere, anywhere],
        out_specs=anywhere,
        out_shape=jax.ShapeDtypeStruct((planes, channels, cells), f32),
        scratch_shapes=[
            pltpu.VMEM((total + 2, width, cells), f32),
            pltpu.VMEM((3, (total + 2) * 9 * width, cells), bf16),
            pltpu.VMEM((3 * width, cells), f32),
            pltpu.VMEM((3, width, taps), f32),
            pltpu.VMEM((3 * width, 27 * width), f32),
            pltpu.VMEM((3, 3 * width, 27 * width), bf16),
            pltpu.VMEM((2, 2, width, cells), f32),
            pltpu.VMEM((2, 2, width, cells), f32),
            pltpu.VMEM((total, width, cells), f32),
            pltpu.VMEM((slots, every, LANES), f32),
            pltpu.VMEM((slots, every, LANES), f32),
            pltpu.VMEM((hidden, every), f32),
            pltpu.VMEM((every, hidden), f32),
            pltpu.VMEM((hidden, every), bf16),
            pltpu.VMEM((hidden, every), bf16),
            pltpu.VMEM((every, hidden), bf16),
            pltpu.VMEM((every, hidden), bf16),
            pltpu.VMEM((every, 2 * LANES), bf16),
            pltpu.VMEM((every, 2 * LANES), bf16),
            pltpu.VMEM((every, 2 * LANES), f32),
            dma((total + 2,)),
            dma((5,)),
            dma((2, groups)),
            dma((groups, planes)),
            dma((2, 2)),
            dma((2, 2)),
            dma((total, tiles)),
            dma((slots,)),
            dma((slots, chan)),
            dma,
        ],
        compiler_params=pltpu.CompilerParams(
            vmem_limit_bytes=LIMIT, collective_id=0, has_side_effects=True
        ),
        name="block",
    )(vin, conv_weight, norm_gain, mlp_in, mlp_out)
    return out.transpose(1, 0, 2)


def solution(mesh):
    in_specs = (P("chan", "depth", None), P(None, None, "chan", None, None), P(), P(), P())
    out_specs = P("chan", "depth", None)
    return jax.shard_map(
        per_device, mesh=mesh, in_specs=in_specs, out_specs=out_specs, check_vma=False
    )
```

```python
import functools

import jax
import jax.numpy as jnp
from jax import lax
from jax.experimental import pallas as pl
from jax.experimental.pallas import tpu as pltpu
from jax.sharding import PartitionSpec as P

W = 32
LANES = 128
LIMIT = 40 * 1024 * 1024
MESH = pl.DeviceIdType.MESH


def split(x):
    hi = x.astype(jnp.bfloat16)
    return hi, (x - hi.astype(jnp.float32)).astype(jnp.bfloat16)


def dot(a, b):
    return jnp.dot(a, b, preferred_element_type=jnp.float32)


def block_body(
    depth, chan, groups, planes, raw, wconv, norm, w_in, w_out, out,
    rows_in, vin, xs, xb, acc, wraw, wf, wmat, edge, halo, ybuf, rin, obuf,
    gain, in_f, out_f, in_hi, in_lo, out_hi, out_lo, r_hi, r_lo, mo,
    raw_sem, x_recv, w_sem, halo_send, swap_send, edge_send, edge_recv,
    y_send, y_recv, o_send, o_recv,
):
    width, cells = xs.shape[1:]
    total = groups * planes
    teams = depth // groups
    tiles = cells // LANES
    rows = chan // tiles
    slots = planes // rows
    channels = groups * width
    part = 3 * width
    span = 3 * part

    d = lax.axis_index("depth")
    c = lax.axis_index("chan")
    j = lax.rem(d, groups)
    t = lax.div(d, groups)
    tile = lax.rem(c, tiles)
    row = lax.div(c, tiles)
    flip = j > 0
    above = lax.rem(t + 1, teams)
    below = lax.rem(t + teams - 1, teams)

    def place(q):
        return jnp.where(flip, total - 1 - q, q)

    raw_load = pltpu.make_async_copy(raw, rows_in, raw_sem)
    raw_load.start()

    barrier = pltpu.get_barrier_semaphore()
    peers = 0
    for team in (above, below) if teams > 2 else (above,):
        for k in range(groups):
            pl.semaphore_signal(barrier, inc=1, device_id={"depth": team * groups + k}, device_id_type=MESH)
            peers += 1
    for g in range(groups):
        for k in range(1 if g == 0 else 0, chan):
            pl.semaphore_signal(
                barrier, inc=1,
                device_id={"depth": t * groups + lax.rem(j + g, groups), "chan": lax.rem(c + k, chan)},
                device_id_type=MESH,
            )
            peers += 1

    loads = [pltpu.make_async_copy(wconv.at[0, l, j], wraw.at[l], w_sem.at[l]) for l in range(3)]
    for load in loads:
        load.start()
    in_load = pltpu.make_async_copy(w_in.at[0], in_f, w_sem.at[3])
    out_load = pltpu.make_async_copy(w_out.at[0], out_f, w_sem.at[4])
    gain_load = pltpu.make_async_copy(norm, gain, w_sem.at[5])
    gain_load.start()
    in_load.start()
    out_load.start()

    raw_load.wait()
    pitch = tiles * planes
    for k in range(groups):
        for z in range(planes):
            for n in range(tiles):
                rows_at = pl.ds(k * width * pitch + n * planes + z, width, stride=pitch)
                vin[k, z, :, n * LANES : (n + 1) * LANES] = rows_in[rows_at, :]
    for z in range(planes):
        slot = j * planes + z + 1
        pltpu.make_async_copy(vin.at[j, z], xs.at[slot], x_recv.at[slot]).start()
    pl.semaphore_wait(barrier, peers)

    def halo_copy(side, k):
        return pltpu.make_async_remote_copy(
            src_ref=vin.at[k, 0 if side == 0 else planes - 1],
            dst_ref=xs.at[total + 1 if side == 0 else 0],
            send_sem=halo_send.at[side, k],
            recv_sem=x_recv.at[total + 1 if side == 0 else 0],
            device_id={"depth": (below if side == 0 else above) * groups + k},
            device_id_type=MESH,
        )

    def swap_copy(k, i):
        peer = lax.rem(j + k, groups)
        z = jnp.where(peer == 0, i, planes - 1 - i)
        slot = j * planes + z + 1
        return pltpu.make_async_remote_copy(
            src_ref=vin.at[peer, z],
            dst_ref=xs.at[slot],
            send_sem=swap_send.at[k, i],
            recv_sem=x_recv.at[slot],
            device_id={"depth": t * groups + peer},
            device_id_type=MESH,
        )

    @pl.when(j == 0)
    def _():
        for k in reversed(range(groups)):
            halo_copy(0, k).start()

    @pl.when(j == groups - 1)
    def _():
        for k in range(groups):
            halo_copy(1, k).start()

    for i in range(planes):
        for k in range(1, groups):
            swap_copy(k, i).start()

    for l in range(3):
        loads[l].wait()
        for b in range(3):
            for e in range(3):
                for a in range(3):
                    start = ((b * 3 + e) * 3 + a) * width
                    piece = wraw[l, :, start : start + width]
                    hi = piece.astype(jnp.bfloat16).astype(jnp.float32)
                    for n, value in enumerate((hi, hi, piece - hi)):
                        col = ((a * 3 + n) * 3 + e) * width
                        wf[b * width : (b + 1) * width, col : col + width] = value
        wmat[l] = wf[...].astype(jnp.bfloat16)

    gain_load.wait()
    in_load.wait()
    out_load.wait()
    hidden = in_f.shape[0]
    step = 64

    def widen(k, _):
        at = pl.ds(pl.multiple_of(k * step, step), step)
        in_hi[at, :], in_lo[at, :] = split(in_f[at, :] * gain[...])
        return 0

    lax.fori_loop(0, hidden // step, widen, 0)

    def widen(k, _):
        at = pl.ds(pl.multiple_of(k * step, step), step)
        out_hi[at, :], out_lo[at, :] = split(out_f[at, :])
        return 0

    lax.fori_loop(0, out_f.shape[0] // step, widen, 0)

    column = lax.broadcasted_iota(jnp.int32, (width, cells), 1) % W

    def prepare(l, slot, x):
        before = jnp.where(column == 0, pltpu.roll(x, cells + 1 - W, 1), pltpu.roll(x, 1, 1))
        after = jnp.where(column == W - 1, pltpu.roll(x, W - 1, 1), pltpu.roll(x, cells - 1, 1))
        for e, value in enumerate((before, x, after)):
            hi, lo = split(value)
            for n, piece in enumerate((hi, lo, hi)):
                at = pl.multiple_of(slot * span + (n * 3 + e) * width, width)
                xb[l, pl.ds(at, width), :] = piece

    def conv(l, p):
        at = pl.ds(pl.multiple_of(p * span, width), 3 * span)
        for n in range(0, cells, 256):
            acc[:, n : n + 256] = dot(wmat[l], xb[l, at, n : n + 256])
        p0, p1, p2 = (acc[b * width : (b + 1) * width, :] for b in range(3))
        return p1 + pltpu.roll(p0, W, 1) + pltpu.roll(p2, cells - W, 1)

    def arrive(q):
        slot = place(q) + 1
        pltpu.make_async_copy(xs.at[slot], xs.at[slot], x_recv.at[slot]).wait()
        prepare(0, slot, xs[slot])

    def edge_copy(l, side):
        front = jnp.where(flip, above, below)
        back = jnp.where(flip, below, above)
        return pltpu.make_async_remote_copy(
            src_ref=edge.at[l, side],
            dst_ref=halo.at[l, 1 - side],
            send_sem=edge_send.at[l, side],
            recv_sem=edge_recv.at[l, 1 - side],
            device_id={"depth": (front if side == 0 else back) * groups + j},
            device_id_type=MESH,
        )

    def send_edge(l, side, u):
        edge[l, side] = u
        edge_copy(l, side).start()

    def take_halo(l, side):
        pltpu.make_async_copy(halo.at[l, side], halo.at[l, side], edge_recv.at[l, side]).wait()
        prepare(l + 1, place(-1 if side == 0 else total) + 1, halo[l, side])

    def inner(l, q):
        p = place(q)
        u = jax.nn.gelu(conv(l, p))
        prepare(l + 1, p + 1, u)
        return u

    def y_target(p, k):
        z = lax.rem(p, planes)
        m = lax.div(p, planes)
        at = lax.rem(tile + tiles // 2 + k, tiles)
        peer = lax.rem(z, rows) * tiles + at
        own = jnp.logical_and(m == j, peer == c)
        src = ybuf.at[p, :, pl.ds(pl.multiple_of(at * LANES, LANES), LANES)]
        slot = lax.div(z, rows)
        first = pl.multiple_of((c * groups + j) * width, width)
        dst = rin.at[slot, pl.ds(first, width), :]
        copy = pltpu.make_async_remote_copy(
            src_ref=src, dst_ref=dst, send_sem=y_send.at[p, k], recv_sem=y_recv.at[slot],
            device_id={"depth": t * groups + m, "chan": peer}, device_id_type=MESH,
        )
        return own, copy, src, dst, y_recv.at[slot]

    def outer(q):
        p = place(q)
        ybuf[p] = xs[p + 1] + conv(2, p)

        def send(k, _):
            own, copy, src, dst, sem = y_target(p, k)

            @pl.when(own)
            def _():
                pltpu.make_async_copy(src, dst, sem).start()

            @pl.when(jnp.logical_not(own))
            def _():
                copy.start()

            return 0

        lax.fori_loop(0, tiles, send, 0)

    arrive(-1)
    arrive(0)

    def wave(i, _):
        arrive(i + 1)
        u = inner(0, i)

        @pl.when(i == 0)
        def _():
            send_edge(0, 0, u)

        @pl.when(i == total - 1)
        def _():
            send_edge(0, 1, u)

        @pl.when(i >= 2)
        def _():
            inner(1, i - 1)

        @pl.when(i >= 4)
        def _():
            outer(i - 2)

        return 0

    lax.fori_loop(0, total, wave, 0)
    take_halo(0, 1)
    send_edge(1, 1, inner(1, total - 1))
    outer(total - 2)
    take_halo(0, 0)
    send_edge(1, 0, inner(1, 0))
    outer(1)
    take_halo(1, 0)
    outer(0)
    take_halo(1, 1)
    outer(total - 1)

    block = min(256, hidden)
    chunks = slots // 2

    def o_target(slot, k):
        peer = lax.rem(c + chan // 2 + k, chan)
        first = pl.multiple_of(peer * channels, channels)
        src = obuf.at[slot, pl.ds(first, channels), :]
        dst = out.at[:, tile * planes + slot * rows + row, 0, :]
        copy = pltpu.make_async_remote_copy(
            src_ref=src, dst_ref=dst, send_sem=o_send.at[slot, k], recv_sem=o_recv,
            device_id={"chan": peer}, device_id_type=MESH,
        )
        return peer == c, copy, src, dst

    def chunk(n, _):
        first = jnp.where(flip, n, chunks - 1 - n) * 2
        for s in range(2):
            pltpu.make_async_copy(rin.at[first + s], rin.at[first + s], y_recv.at[first + s]).wait()
            x = rin[first + s]
            r = x * lax.rsqrt(jnp.mean(x * x, axis=0, keepdims=True) + 1e-06)
            at = slice(s * LANES, (s + 1) * LANES)
            r_hi[:, at], r_lo[:, at] = split(r)
            mo[:, at] = x

        def mix(k, _):
            at = pl.ds(pl.multiple_of(k * block, block), block)
            h = dot(in_hi[at, :], r_hi[...]) + (dot(in_hi[at, :], r_lo[...]) + dot(in_lo[at, :], r_hi[...]))
            h_hi, h_lo = split(jax.nn.gelu(h))
            mo[...] += dot(out_hi[:, at], h_hi) + (dot(out_hi[:, at], h_lo) + dot(out_lo[:, at], h_hi))
            return 0

        lax.fori_loop(0, hidden // block, mix, 0)
        for s in range(2):
            obuf[first + s] = mo[:, s * LANES : (s + 1) * LANES]

            def send(k, _):
                own, copy, src, dst = o_target(first + s, k)

                @pl.when(own)
                def _():
                    pltpu.make_async_copy(src, dst, o_recv).start()

                @pl.when(jnp.logical_not(own))
                def _():
                    copy.start()

                return 0

            lax.fori_loop(0, chan, send, 0)
        return 0

    lax.fori_loop(0, chunks, chunk, 0)

    @pl.when(j == 0)
    def _():
        for k in range(groups):
            halo_copy(0, k).wait_send()

    @pl.when(j == groups - 1)
    def _():
        for k in range(groups):
            halo_copy(1, k).wait_send()

    for i in range(planes):
        for k in range(1, groups):
            swap_copy(k, i).wait_send()
    for l in range(2):
        for side in range(2):
            edge_copy(l, side).wait_send()

    def drain(n, _):
        own, copy, *_ = y_target(lax.div(n, tiles), lax.rem(n, tiles))

        @pl.when(jnp.logical_not(own))
        def _():
            copy.wait_send()

        return 0

    lax.fori_loop(0, total * tiles, drain, 0)

    def drain(n, _):
        own, copy, *_ = o_target(lax.div(n, chan), lax.rem(n, chan))

        @pl.when(jnp.logical_not(own))
        def _():
            copy.wait_send()

        return 0

    lax.fori_loop(0, slots * chan, drain, 0)
    pltpu.make_async_copy(out, out, o_recv).wait()


def per_device(volume, conv_weight, norm_gain, mlp_in, mlp_out):
    channels, planes, cells = volume.shape
    width, taps = conv_weight.shape[-2:]
    groups = channels // width
    depth, chan = lax.axis_size("depth"), lax.axis_size("chan")
    total = groups * planes
    tiles = cells // LANES
    slots = planes // (chan // tiles)
    hidden, every = mlp_in.shape[1:]
    raw = volume.reshape(channels, planes, tiles, LANES).transpose(0, 2, 1, 3).reshape(-1, LANES)
    f32, bf16 = jnp.float32, jnp.bfloat16
    dma = pltpu.SemaphoreType.DMA
    keep = functools.partial(pltpu.with_memory_space_constraint, memory_space=pltpu.HBM)
    far = pl.BlockSpec(memory_space=pltpu.HBM)
    out = pl.pallas_call(
        functools.partial(block_body, depth, chan, groups, planes),
        in_specs=[far] * 5,
        out_specs=pl.BlockSpec(memory_space=pl.ANY),
        out_shape=jax.ShapeDtypeStruct((channels, tiles * planes, 1, LANES), f32),
        scratch_shapes=[
            pltpu.VMEM(raw.shape, f32),
            pltpu.VMEM((groups, planes, width, cells), f32),
            pltpu.VMEM((total + 2, width, cells), f32),
            pltpu.VMEM((3, (total + 2) * 9 * width, cells), bf16),
            pltpu.VMEM((3 * width, cells), f32),
            pltpu.VMEM((3, width, taps), f32),
            pltpu.VMEM((3 * width, 27 * width), f32),
            pltpu.VMEM((3, 3 * width, 27 * width), bf16),
            pltpu.VMEM((2, 2, width, cells), f32),
            pltpu.VMEM((2, 2, width, cells), f32),
            pltpu.VMEM((total, width, cells), f32),
            pltpu.VMEM((slots, every, LANES), f32),
            pltpu.VMEM((slots, every, LANES), f32),
            pltpu.VMEM((1, every), f32),
            pltpu.VMEM((hidden, every), f32),
            pltpu.VMEM((every, hidden), f32),
            pltpu.VMEM((hidden, every), bf16),
            pltpu.VMEM((hidden, every), bf16),
            pltpu.VMEM((every, hidden), bf16),
            pltpu.VMEM((every, hidden), bf16),
            pltpu.VMEM((every, 2 * LANES), bf16),
            pltpu.VMEM((every, 2 * LANES), bf16),
            pltpu.VMEM((every, 2 * LANES), f32),
            dma,
            dma((total + 2,)),
            dma((6,)),
            dma((2, groups)),
            dma((groups, planes)),
            dma((2, 2)),
            dma((2, 2)),
            dma((total, tiles)),
            dma((slots,)),
            dma((slots, chan)),
            dma,
        ],
        compiler_params=pltpu.CompilerParams(
            vmem_limit_bytes=LIMIT, collective_id=0, has_side_effects=True
        ),
        name="block",
    )(keep(raw), keep(conv_weight), keep(norm_gain), keep(mlp_in), keep(mlp_out))
    out = out.reshape(channels, tiles, planes, LANES).transpose(0, 2, 1, 3)
    return out.reshape(volume.shape)


def solution(mesh):
    in_specs = (P("chan", "depth", None), P(None, None, "chan", None, None), P(), P(), P())
    out_specs = P("chan", "depth", None)
    return jax.shard_map(
        per_device, mesh=mesh, in_specs=in_specs, out_specs=out_specs, check_vma=False
    )
```

```python
import functools

import jax
import jax.numpy as jnp
from jax import lax
from jax.experimental import pallas as pl
from jax.experimental.pallas import tpu as pltpu
from jax.sharding import PartitionSpec as P

W = 32
LANES = 128
LIMIT = 40 * 1024 * 1024
MESH = pl.DeviceIdType.MESH


def split(x):
    hi = x.astype(jnp.bfloat16)
    return hi, (x - hi.astype(jnp.float32)).astype(jnp.bfloat16)


def dot(a, b):
    return jnp.dot(a, b, preferred_element_type=jnp.float32)


def block_body(
    depth, chan, groups, planes, raw, wconv, norm, w_in, w_out, out,
    rows_in, vin, xs, xb, acc, wraw, wf, wmat, edge, halo, ybuf, rin, obuf,
    gain, in_f, out_f, in_hi, in_lo, out_hi, out_lo, r_hi, r_lo, mo,
    raw_sem, x_recv, w_sem, halo_send, swap_send, edge_send, edge_recv,
    y_send, y_recv, o_send, o_recv,
):
    width, cells = xs.shape[1:]
    total = groups * planes
    teams = depth // groups
    tiles = cells // LANES
    rows = chan // tiles
    slots = planes // rows
    channels = groups * width
    part = 3 * width
    span = 3 * part

    d = lax.axis_index("depth")
    c = lax.axis_index("chan")
    j = lax.rem(d, groups)
    t = lax.div(d, groups)
    tile = lax.rem(c, tiles)
    row = lax.div(c, tiles)
    flip = j > 0
    above = lax.rem(t + 1, teams)
    below = lax.rem(t + teams - 1, teams)

    def place(q):
        return jnp.where(flip, total - 1 - q, q)

    raw_load = pltpu.make_async_copy(raw, rows_in, raw_sem)
    raw_load.start()

    barrier = pltpu.get_barrier_semaphore()
    peers = 0
    for team in (above, below) if teams > 2 else (above,):
        for k in range(groups):
            pl.semaphore_signal(barrier, inc=1, device_id={"depth": team * groups + k}, device_id_type=MESH)
            peers += 1
    for g in range(groups):
        for k in range(1 if g == 0 else 0, chan):
            pl.semaphore_signal(
                barrier, inc=1,
                device_id={"depth": t * groups + lax.rem(j + g, groups), "chan": lax.rem(c + k, chan)},
                device_id_type=MESH,
            )
            peers += 1

    loads = [pltpu.make_async_copy(wconv.at[0, l, j], wraw.at[l], w_sem.at[l]) for l in range(3)]
    for load in loads:
        load.start()
    in_load = pltpu.make_async_copy(w_in.at[0], in_f, w_sem.at[3])
    out_load = pltpu.make_async_copy(w_out.at[0], out_f, w_sem.at[4])
    gain_load = pltpu.make_async_copy(norm, gain, w_sem.at[5])
    gain_load.start()
    in_load.start()
    out_load.start()

    def halo_copy(side, k):
        return pltpu.make_async_remote_copy(
            src_ref=vin.at[k, 0 if side == 0 else planes - 1],
            dst_ref=xs.at[total + 1 if side == 0 else 0],
            send_sem=halo_send.at[side, k],
            recv_sem=x_recv.at[total + 1 if side == 0 else 0],
            device_id={"depth": (below if side == 0 else above) * groups + k},
            device_id_type=MESH,
        )

    def swap_plane(k, i):
        peer = lax.rem(j + k, groups)
        return peer, jnp.where(peer == 0, i, planes - 1 - i)

    def swap_copy(k, i):
        peer, z = swap_plane(k, i)
        slot = j * planes + z + 1
        return pltpu.make_async_remote_copy(
            src_ref=vin.at[peer, z],
            dst_ref=xs.at[slot],
            send_sem=swap_send.at[k, i],
            recv_sem=x_recv.at[slot],
            device_id={"depth": t * groups + peer},
            device_id_type=MESH,
        )

    pitch = tiles * planes

    def fetch(k, z):
        for n in range(tiles):
            at = pl.ds(k * width * pitch + n * planes + z, width, stride=pitch)
            vin[k, z, :, n * LANES : (n + 1) * LANES] = rows_in[at, :]

    def halo_start(low, high):
        @pl.when(j == 0)
        def _():
            for k in low:
                halo_copy(0, k).start()

        @pl.when(j == groups - 1)
        def _():
            for k in high:
                halo_copy(1, k).start()

    def keep(z):
        slot = j * planes + z + 1
        pltpu.make_async_copy(vin.at[j, z], xs.at[slot], x_recv.at[slot]).start()

    raw_load.wait()
    if groups == 2:
        other = 1 - j
        fetch(other, jnp.where(j == 0, 0, planes - 1))
        pl.semaphore_wait(barrier, peers)
        halo_start([1], [0])
        for i in range(planes):
            if i < planes - 1:
                fetch(*swap_plane(1, i))
            swap_copy(1, i).start()
        for z in range(planes):
            fetch(j, z)
            keep(z)
        halo_start([0], [1])
    else:
        for k in range(groups):
            for z in range(planes):
                fetch(k, z)
        pl.semaphore_wait(barrier, peers)
        halo_start(range(groups), range(groups))
        for i in range(planes):
            for k in range(1, groups):
                swap_copy(k, i).start()
        for z in range(planes):
            keep(z)

    for l in range(3):
        loads[l].wait()
        for b in range(3):
            for e in range(3):
                for a in range(3):
                    start = ((b * 3 + e) * 3 + a) * width
                    piece = wraw[l, :, start : start + width]
                    hi = piece.astype(jnp.bfloat16).astype(jnp.float32)
                    for n, value in enumerate((hi, hi, piece - hi)):
                        col = ((a * 3 + n) * 3 + e) * width
                        wf[b * width : (b + 1) * width, col : col + width] = value
        wmat[l] = wf[...].astype(jnp.bfloat16)

    column = lax.broadcasted_iota(jnp.int32, (width, cells), 1) % W

    def prepare(l, slot, x):
        before = jnp.where(column == 0, pltpu.roll(x, cells + 1 - W, 1), pltpu.roll(x, 1, 1))
        after = jnp.where(column == W - 1, pltpu.roll(x, W - 1, 1), pltpu.roll(x, cells - 1, 1))
        for e, value in enumerate((before, x, after)):
            hi, lo = split(value)
            for n, piece in enumerate((hi, lo, hi)):
                at = pl.multiple_of(slot * span + (n * 3 + e) * width, width)
                xb[l, pl.ds(at, width), :] = piece

    def conv(l, p):
        at = pl.ds(pl.multiple_of(p * span, width), 3 * span)
        for n in range(0, cells, 256):
            acc[:, n : n + 256] = dot(wmat[l], xb[l, at, n : n + 256])
        p0, p1, p2 = (acc[b * width : (b + 1) * width, :] for b in range(3))
        return p1 + pltpu.roll(p0, W, 1) + pltpu.roll(p2, cells - W, 1)

    def arrive(q):
        slot = place(q) + 1
        pltpu.make_async_copy(xs.at[slot], xs.at[slot], x_recv.at[slot]).wait()
        prepare(0, slot, xs[slot])

    def edge_copy(l, side):
        front = jnp.where(flip, above, below)
        back = jnp.where(flip, below, above)
        return pltpu.make_async_remote_copy(
            src_ref=edge.at[l, side],
            dst_ref=halo.at[l, 1 - side],
            send_sem=edge_send.at[l, side],
            recv_sem=edge_recv.at[l, 1 - side],
            device_id={"depth": (front if side == 0 else back) * groups + j},
            device_id_type=MESH,
        )

    def send_edge(l, side, u):
        edge[l, side] = u
        edge_copy(l, side).start()

    def take_halo(l, side):
        pltpu.make_async_copy(halo.at[l, side], halo.at[l, side], edge_recv.at[l, side]).wait()
        prepare(l + 1, place(-1 if side == 0 else total) + 1, halo[l, side])

    def inner(l, q):
        p = place(q)
        u = jax.nn.gelu(conv(l, p))
        prepare(l + 1, p + 1, u)
        return u

    def y_target(p, k):
        z = lax.rem(p, planes)
        m = lax.div(p, planes)
        at = lax.rem(tile + tiles // 2 + k, tiles)
        peer = lax.rem(z, rows) * tiles + at
        own = jnp.logical_and(m == j, peer == c)
        src = ybuf.at[p, :, pl.ds(pl.multiple_of(at * LANES, LANES), LANES)]
        slot = lax.div(z, rows)
        first = pl.multiple_of((c * groups + j) * width, width)
        dst = rin.at[slot, pl.ds(first, width), :]
        copy = pltpu.make_async_remote_copy(
            src_ref=src, dst_ref=dst, send_sem=y_send.at[p, k], recv_sem=y_recv.at[slot],
            device_id={"depth": t * groups + m, "chan": peer}, device_id_type=MESH,
        )
        return own, copy, src, dst, y_recv.at[slot]

    def outer(q):
        p = place(q)
        ybuf[p] = xs[p + 1] + conv(2, p)

        def send(k, _):
            own, copy, src, dst, sem = y_target(p, k)

            @pl.when(own)
            def _():
                pltpu.make_async_copy(src, dst, sem).start()

            @pl.when(jnp.logical_not(own))
            def _():
                copy.start()

            return 0

        lax.fori_loop(0, tiles, send, 0)

    def own(q, _):
        arrive(q)
        return 0

    def first(q, _):
        inner(0, q)
        return 0

    def second(q, _):
        inner(1, q)
        return 0

    lax.fori_loop(0, planes, own, 0)
    lax.fori_loop(1, planes - 1, first, 0)
    arrive(-1)
    send_edge(0, 0, inner(0, 0))
    lax.fori_loop(1, planes - 2, second, 0)

    def wave(i, _):
        arrive(i + 1)
        u = inner(0, i)

        @pl.when(i == total - 1)
        def _():
            send_edge(0, 1, u)

        inner(1, i - 1)

        @pl.when(i >= 4)
        def _():
            outer(i - 2)

        return 0

    lax.fori_loop(planes - 1, total, wave, 0)
    take_halo(0, 1)
    send_edge(1, 1, inner(1, total - 1))
    outer(total - 2)
    gain_load.wait()
    in_load.wait()
    out_load.wait()
    hidden = in_f.shape[0]
    step = 64

    def widen(k, _):
        at = pl.ds(pl.multiple_of(k * step, step), step)
        in_hi[at, :], in_lo[at, :] = split(in_f[at, :] * gain[...])
        return 0

    lax.fori_loop(0, hidden // step, widen, 0)

    def widen(k, _):
        at = pl.ds(pl.multiple_of(k * step, step), step)
        out_hi[at, :], out_lo[at, :] = split(out_f[at, :])
        return 0

    lax.fori_loop(0, out_f.shape[0] // step, widen, 0)

    take_halo(0, 0)
    send_edge(1, 0, inner(1, 0))
    outer(1)
    take_halo(1, 0)
    outer(0)
    take_halo(1, 1)
    outer(total - 1)

    block = min(256, hidden)
    chunks = slots // 2

    def o_target(slot, k):
        peer = lax.rem(c + chan // 2 + k, chan)
        first = pl.multiple_of(peer * channels, channels)
        src = obuf.at[slot, pl.ds(first, channels), :]
        dst = out.at[:, tile * planes + slot * rows + row, 0, :]
        copy = pltpu.make_async_remote_copy(
            src_ref=src, dst_ref=dst, send_sem=o_send.at[slot, k], recv_sem=o_recv,
            device_id={"chan": peer}, device_id_type=MESH,
        )
        return peer == c, copy, src, dst

    def chunk(n, _):
        first = jnp.where(flip, n, chunks - 1 - n) * 2
        for s in range(2):
            pltpu.make_async_copy(rin.at[first + s], rin.at[first + s], y_recv.at[first + s]).wait()
            x = rin[first + s]
            r = x * lax.rsqrt(jnp.mean(x * x, axis=0, keepdims=True) + 1e-06)
            at = slice(s * LANES, (s + 1) * LANES)
            r_hi[:, at], r_lo[:, at] = split(r)
            mo[:, at] = x

        def mix(k, _):
            at = pl.ds(pl.multiple_of(k * block, block), block)
            h = dot(in_hi[at, :], r_hi[...]) + (dot(in_hi[at, :], r_lo[...]) + dot(in_lo[at, :], r_hi[...]))
            h_hi, h_lo = split(jax.nn.gelu(h))
            mo[...] += dot(out_hi[:, at], h_hi) + (dot(out_hi[:, at], h_lo) + dot(out_lo[:, at], h_hi))
            return 0

        lax.fori_loop(0, hidden // block, mix, 0)
        for s in range(2):
            obuf[first + s] = mo[:, s * LANES : (s + 1) * LANES]

            def send(k, _):
                own, copy, src, dst = o_target(first + s, k)

                @pl.when(own)
                def _():
                    pltpu.make_async_copy(src, dst, o_recv).start()

                @pl.when(jnp.logical_not(own))
                def _():
                    copy.start()

                return 0

            lax.fori_loop(0, chan, send, 0)
        return 0

    lax.fori_loop(0, chunks, chunk, 0)

    @pl.when(j == 0)
    def _():
        for k in range(groups):
            halo_copy(0, k).wait_send()

    @pl.when(j == groups - 1)
    def _():
        for k in range(groups):
            halo_copy(1, k).wait_send()

    for i in range(planes):
        for k in range(1, groups):
            swap_copy(k, i).wait_send()
    for l in range(2):
        for side in range(2):
            edge_copy(l, side).wait_send()

    def drain(n, _):
        own, copy, *_ = y_target(lax.div(n, tiles), lax.rem(n, tiles))

        @pl.when(jnp.logical_not(own))
        def _():
            copy.wait_send()

        return 0

    lax.fori_loop(0, total * tiles, drain, 0)

    def drain(n, _):
        own, copy, *_ = o_target(lax.div(n, chan), lax.rem(n, chan))

        @pl.when(jnp.logical_not(own))
        def _():
            copy.wait_send()

        return 0

    lax.fori_loop(0, slots * chan, drain, 0)
    pltpu.make_async_copy(out, out, o_recv).wait()


def per_device(volume, conv_weight, norm_gain, mlp_in, mlp_out):
    channels, planes, cells = volume.shape
    width, taps = conv_weight.shape[-2:]
    groups = channels // width
    depth, chan = lax.axis_size("depth"), lax.axis_size("chan")
    total = groups * planes
    tiles = cells // LANES
    slots = planes // (chan // tiles)
    hidden, every = mlp_in.shape[1:]
    raw = volume.reshape(channels, planes, tiles, LANES).transpose(0, 2, 1, 3).reshape(-1, LANES)
    f32, bf16 = jnp.float32, jnp.bfloat16
    dma = pltpu.SemaphoreType.DMA
    keep = functools.partial(pltpu.with_memory_space_constraint, memory_space=pltpu.HBM)
    far = pl.BlockSpec(memory_space=pltpu.HBM)
    out = pl.pallas_call(
        functools.partial(block_body, depth, chan, groups, planes),
        in_specs=[far] * 5,
        out_specs=pl.BlockSpec(memory_space=pl.ANY),
        out_shape=jax.ShapeDtypeStruct((channels, tiles * planes, 1, LANES), f32),
        scratch_shapes=[
            pltpu.VMEM(raw.shape, f32),
            pltpu.VMEM((groups, planes, width, cells), f32),
            pltpu.VMEM((total + 2, width, cells), f32),
            pltpu.VMEM((3, (total + 2) * 9 * width, cells), bf16),
            pltpu.VMEM((3 * width, cells), f32),
            pltpu.VMEM((3, width, taps), f32),
            pltpu.VMEM((3 * width, 27 * width), f32),
            pltpu.VMEM((3, 3 * width, 27 * width), bf16),
            pltpu.VMEM((2, 2, width, cells), f32),
            pltpu.VMEM((2, 2, width, cells), f32),
            pltpu.VMEM((total, width, cells), f32),
            pltpu.VMEM((slots, every, LANES), f32),
            pltpu.VMEM((slots, every, LANES), f32),
            pltpu.VMEM((1, every), f32),
            pltpu.VMEM((hidden, every), f32),
            pltpu.VMEM((every, hidden), f32),
            pltpu.VMEM((hidden, every), bf16),
            pltpu.VMEM((hidden, every), bf16),
            pltpu.VMEM((every, hidden), bf16),
            pltpu.VMEM((every, hidden), bf16),
            pltpu.VMEM((every, 2 * LANES), bf16),
            pltpu.VMEM((every, 2 * LANES), bf16),
            pltpu.VMEM((every, 2 * LANES), f32),
            dma,
            dma((total + 2,)),
            dma((6,)),
            dma((2, groups)),
            dma((groups, planes)),
            dma((2, 2)),
            dma((2, 2)),
            dma((total, tiles)),
            dma((slots,)),
            dma((slots, chan)),
            dma,
        ],
        compiler_params=pltpu.CompilerParams(
            vmem_limit_bytes=LIMIT, collective_id=0, has_side_effects=True
        ),
        name="block",
    )(keep(raw), keep(conv_weight), keep(norm_gain), keep(mlp_in), keep(mlp_out))
    out = out.reshape(channels, tiles, planes, LANES).transpose(0, 2, 1, 3)
    return out.reshape(volume.shape)


def solution(mesh):
    in_specs = (P("chan", "depth", None), P(None, None, "chan", None, None), P(), P(), P())
    out_specs = P("chan", "depth", None)
    return jax.shard_map(
        per_device, mesh=mesh, in_specs=in_specs, out_specs=out_specs, check_vma=False
    )
```

```python
import functools

import jax
import jax.numpy as jnp
from jax import lax
from jax.experimental import pallas as pl
from jax.experimental.pallas import tpu as pltpu
from jax.sharding import PartitionSpec as P

W = 32
LANES = 128
LIMIT = 40 * 1024 * 1024
MESH = pl.DeviceIdType.MESH


def split(x):
    hi = x.astype(jnp.bfloat16)
    return hi, (x - hi.astype(jnp.float32)).astype(jnp.bfloat16)


def dot(a, b):
    return jnp.dot(a, b, preferred_element_type=jnp.float32)


def block_body(
    depth, chan, groups, planes, raw, wconv, norm, w_in, w_out, out,
    rows_in, vin, xs, xb, acc, wraw, wf, wmat, edge, halo, ybuf, rin, obuf,
    gain, in_f, out_f, in_hi, in_lo, out_hi, out_lo, r_hi, r_lo, mo,
    raw_sem, x_recv, w_sem, halo_send, swap_send, edge_send, edge_recv,
    y_send, y_recv, o_send, o_recv,
):
    width, cells = xs.shape[1:]
    total = groups * planes
    teams = depth // groups
    tiles = cells // LANES
    rows = chan // tiles
    slots = planes // rows
    channels = groups * width
    part = 3 * width
    span = 3 * part

    d = lax.axis_index("depth")
    c = lax.axis_index("chan")
    j = lax.rem(d, groups)
    t = lax.div(d, groups)
    tile = lax.rem(c, tiles)
    row = lax.div(c, tiles)
    flip = j > 0
    above = lax.rem(t + 1, teams)
    below = lax.rem(t + teams - 1, teams)

    def place(q):
        return jnp.where(flip, total - 1 - q, q)

    raw_load = pltpu.make_async_copy(raw, rows_in, raw_sem)
    raw_load.start()

    barrier = pltpu.get_barrier_semaphore()
    peers = 0
    for team in (above, below) if teams > 2 else (above,):
        for k in range(groups):
            pl.semaphore_signal(barrier, inc=1, device_id={"depth": team * groups + k}, device_id_type=MESH)
            peers += 1
    for g in range(groups):
        for k in range(1 if g == 0 else 0, chan):
            pl.semaphore_signal(
                barrier, inc=1,
                device_id={"depth": t * groups + lax.rem(j + g, groups), "chan": lax.rem(c + k, chan)},
                device_id_type=MESH,
            )
            peers += 1

    loads = [pltpu.make_async_copy(wconv.at[0, l, j], wraw.at[l], w_sem.at[l]) for l in range(3)]
    for load in loads:
        load.start()
    in_load = pltpu.make_async_copy(w_in.at[0], in_f, w_sem.at[3])
    out_load = pltpu.make_async_copy(w_out.at[0], out_f, w_sem.at[4])
    gain_load = pltpu.make_async_copy(norm, gain, w_sem.at[5])
    gain_load.start()
    in_load.start()
    out_load.start()

    def halo_copy(side, k):
        return pltpu.make_async_remote_copy(
            src_ref=vin.at[k, 0 if side == 0 else planes - 1],
            dst_ref=xs.at[total + 1 if side == 0 else 0],
            send_sem=halo_send.at[side, k],
            recv_sem=x_recv.at[total + 1 if side == 0 else 0],
            device_id={"depth": (below if side == 0 else above) * groups + k},
            device_id_type=MESH,
        )

    def swap_plane(k, i):
        peer = lax.rem(j + k, groups)
        return peer, jnp.where(peer == 0, i, planes - 1 - i)

    def swap_copy(k, i):
        peer, z = swap_plane(k, i)
        slot = j * planes + z + 1
        return pltpu.make_async_remote_copy(
            src_ref=vin.at[peer, z],
            dst_ref=xs.at[slot],
            send_sem=swap_send.at[k, i],
            recv_sem=x_recv.at[slot],
            device_id={"depth": t * groups + peer},
            device_id_type=MESH,
        )

    pitch = tiles * planes

    def fetch(k, z):
        for n in range(tiles):
            at = pl.ds(k * width * pitch + n * planes + z, width, stride=pitch)
            vin[k, z, :, n * LANES : (n + 1) * LANES] = rows_in[at, :]

    def halo_start(low, high):
        @pl.when(j == 0)
        def _():
            for k in low:
                halo_copy(0, k).start()

        @pl.when(j == groups - 1)
        def _():
            for k in high:
                halo_copy(1, k).start()

    def keep(z):
        slot = j * planes + z + 1
        pltpu.make_async_copy(vin.at[j, z], xs.at[slot], x_recv.at[slot]).start()

    raw_load.wait()
    if groups == 2:
        fetch(*swap_plane(1, 0))
        pl.semaphore_wait(barrier, peers)
        for i in range(planes):
            if i > 0:
                fetch(*swap_plane(1, i))
            swap_copy(1, i).start()
        halo_start([1], [0])
        for z in range(planes):
            fetch(j, z)
            keep(z)
        halo_start([0], [1])
    else:
        for k in range(groups):
            for z in range(planes):
                fetch(k, z)
        pl.semaphore_wait(barrier, peers)
        halo_start(range(groups), range(groups))
        for i in range(planes):
            for k in range(1, groups):
                swap_copy(k, i).start()
        for z in range(planes):
            keep(z)

    for l in range(3):
        loads[l].wait()
        for b in range(3):
            for e in range(3):
                for a in range(3):
                    start = ((b * 3 + e) * 3 + a) * width
                    piece = wraw[l, :, start : start + width]
                    hi = piece.astype(jnp.bfloat16).astype(jnp.float32)
                    for n, value in enumerate((hi, hi, piece - hi)):
                        col = ((a * 3 + n) * 3 + e) * width
                        wf[b * width : (b + 1) * width, col : col + width] = value
        wmat[l] = wf[...].astype(jnp.bfloat16)

    column = lax.broadcasted_iota(jnp.int32, (width, cells), 1) % W

    def prepare(l, slot, x):
        before = jnp.where(column == 0, pltpu.roll(x, cells + 1 - W, 1), pltpu.roll(x, 1, 1))
        after = jnp.where(column == W - 1, pltpu.roll(x, W - 1, 1), pltpu.roll(x, cells - 1, 1))
        for e, value in enumerate((before, x, after)):
            hi, lo = split(value)
            for n, piece in enumerate((hi, lo, hi)):
                at = pl.multiple_of(slot * span + (n * 3 + e) * width, width)
                xb[l, pl.ds(at, width), :] = piece

    def conv(l, p):
        at = pl.ds(pl.multiple_of(p * span, width), 3 * span)
        for n in range(0, cells, 256):
            acc[:, n : n + 256] = dot(wmat[l], xb[l, at, n : n + 256])
        p0, p1, p2 = (acc[b * width : (b + 1) * width, :] for b in range(3))
        return p1 + pltpu.roll(p0, W, 1) + pltpu.roll(p2, cells - W, 1)

    def arrive(q):
        slot = place(q) + 1
        pltpu.make_async_copy(xs.at[slot], xs.at[slot], x_recv.at[slot]).wait()
        prepare(0, slot, xs[slot])

    def edge_copy(l, side):
        front = jnp.where(flip, above, below)
        back = jnp.where(flip, below, above)
        return pltpu.make_async_remote_copy(
            src_ref=edge.at[l, side],
            dst_ref=halo.at[l, 1 - side],
            send_sem=edge_send.at[l, side],
            recv_sem=edge_recv.at[l, 1 - side],
            device_id={"depth": (front if side == 0 else back) * groups + j},
            device_id_type=MESH,
        )

    def send_edge(l, side, u):
        edge[l, side] = u
        edge_copy(l, side).start()

    def take_halo(l, side):
        pltpu.make_async_copy(halo.at[l, side], halo.at[l, side], edge_recv.at[l, side]).wait()
        prepare(l + 1, place(-1 if side == 0 else total) + 1, halo[l, side])

    def inner(l, q):
        p = place(q)
        u = jax.nn.gelu(conv(l, p))
        prepare(l + 1, p + 1, u)
        return u

    def y_target(p, k):
        z = lax.rem(p, planes)
        m = lax.div(p, planes)
        at = lax.rem(tile + tiles // 2 + k, tiles)
        peer = lax.rem(z, rows) * tiles + at
        own = jnp.logical_and(m == j, peer == c)
        src = ybuf.at[p, :, pl.ds(pl.multiple_of(at * LANES, LANES), LANES)]
        slot = lax.div(z, rows)
        first = pl.multiple_of((c * groups + j) * width, width)
        dst = rin.at[slot, pl.ds(first, width), :]
        copy = pltpu.make_async_remote_copy(
            src_ref=src, dst_ref=dst, send_sem=y_send.at[p, k], recv_sem=y_recv.at[slot],
            device_id={"depth": t * groups + m, "chan": peer}, device_id_type=MESH,
        )
        return own, copy, src, dst, y_recv.at[slot]

    def outer(q):
        p = place(q)
        ybuf[p] = xs[p + 1] + conv(2, p)

        def send(k, _):
            own, copy, src, dst, sem = y_target(p, k)

            @pl.when(own)
            def _():
                pltpu.make_async_copy(src, dst, sem).start()

            @pl.when(jnp.logical_not(own))
            def _():
                copy.start()

            return 0

        lax.fori_loop(0, tiles, send, 0)

    def own(q, _):
        arrive(q)
        return 0

    def first(q, _):
        inner(0, q)
        return 0

    lax.fori_loop(0, planes, own, 0)
    lax.fori_loop(1, planes - 1, first, 0)
    def wave(i, _):
        arrive(i + 1)
        u = inner(0, i)

        @pl.when(i == total - 1)
        def _():
            send_edge(0, 1, u)

        inner(1, i - 1)

        @pl.when(i >= 5)
        def _():
            outer(i - 2)

        return 0

    lax.fori_loop(planes - 1, total, wave, 0)
    arrive(-1)
    send_edge(0, 0, inner(0, 0))
    inner(1, 1)
    if total > 4:
        outer(2)
    take_halo(0, 0)
    send_edge(1, 0, inner(1, 0))
    outer(1)
    gain_load.wait()
    in_load.wait()
    out_load.wait()
    hidden = in_f.shape[0]
    step = 64

    def widen(k, _):
        at = pl.ds(pl.multiple_of(k * step, step), step)
        in_hi[at, :], in_lo[at, :] = split(in_f[at, :] * gain[...])
        return 0

    lax.fori_loop(0, hidden // step, widen, 0)

    def widen(k, _):
        at = pl.ds(pl.multiple_of(k * step, step), step)
        out_hi[at, :], out_lo[at, :] = split(out_f[at, :])
        return 0

    lax.fori_loop(0, out_f.shape[0] // step, widen, 0)

    take_halo(0, 1)
    send_edge(1, 1, inner(1, total - 1))
    outer(total - 2)
    take_halo(1, 1)
    outer(total - 1)
    take_halo(1, 0)
    outer(0)

    block = min(256, hidden)
    chunks = slots // 2

    def o_target(slot, k):
        peer = lax.rem(c + chan // 2 + k, chan)
        first = pl.multiple_of(peer * channels, channels)
        src = obuf.at[slot, pl.ds(first, channels), :]
        dst = out.at[:, tile * planes + slot * rows + row, 0, :]
        copy = pltpu.make_async_remote_copy(
            src_ref=src, dst_ref=dst, send_sem=o_send.at[slot, k], recv_sem=o_recv,
            device_id={"chan": peer}, device_id_type=MESH,
        )
        return peer == c, copy, src, dst

    def chunk(n, _):
        first = jnp.where(flip, n, chunks - 1 - n) * 2
        for s in range(2):
            pltpu.make_async_copy(rin.at[first + s], rin.at[first + s], y_recv.at[first + s]).wait()
            x = rin[first + s]
            r = x * lax.rsqrt(jnp.mean(x * x, axis=0, keepdims=True) + 1e-06)
            at = slice(s * LANES, (s + 1) * LANES)
            r_hi[:, at], r_lo[:, at] = split(r)
            mo[:, at] = x

        def mix(k, _):
            at = pl.ds(pl.multiple_of(k * block, block), block)
            h = dot(in_hi[at, :], r_hi[...]) + (dot(in_hi[at, :], r_lo[...]) + dot(in_lo[at, :], r_hi[...]))
            h_hi, h_lo = split(jax.nn.gelu(h))
            mo[...] += dot(out_hi[:, at], h_hi) + (dot(out_hi[:, at], h_lo) + dot(out_lo[:, at], h_hi))
            return 0

        lax.fori_loop(0, hidden // block, mix, 0)
        for s in range(2):
            obuf[first + s] = mo[:, s * LANES : (s + 1) * LANES]

            def send(k, _):
                own, copy, src, dst = o_target(first + s, k)

                @pl.when(own)
                def _():
                    pltpu.make_async_copy(src, dst, o_recv).start()

                @pl.when(jnp.logical_not(own))
                def _():
                    copy.start()

                return 0

            lax.fori_loop(0, chan, send, 0)
        return 0

    lax.fori_loop(0, chunks, chunk, 0)

    @pl.when(j == 0)
    def _():
        for k in range(groups):
            halo_copy(0, k).wait_send()

    @pl.when(j == groups - 1)
    def _():
        for k in range(groups):
            halo_copy(1, k).wait_send()

    for i in range(planes):
        for k in range(1, groups):
            swap_copy(k, i).wait_send()
    for l in range(2):
        for side in range(2):
            edge_copy(l, side).wait_send()

    def drain(n, _):
        own, copy, *_ = y_target(lax.div(n, tiles), lax.rem(n, tiles))

        @pl.when(jnp.logical_not(own))
        def _():
            copy.wait_send()

        return 0

    lax.fori_loop(0, total * tiles, drain, 0)

    def drain(n, _):
        own, copy, *_ = o_target(lax.div(n, chan), lax.rem(n, chan))

        @pl.when(jnp.logical_not(own))
        def _():
            copy.wait_send()

        return 0

    lax.fori_loop(0, slots * chan, drain, 0)
    pltpu.make_async_copy(out, out, o_recv).wait()


def per_device(volume, conv_weight, norm_gain, mlp_in, mlp_out):
    channels, planes, cells = volume.shape
    width, taps = conv_weight.shape[-2:]
    groups = channels // width
    depth, chan = lax.axis_size("depth"), lax.axis_size("chan")
    total = groups * planes
    tiles = cells // LANES
    slots = planes // (chan // tiles)
    hidden, every = mlp_in.shape[1:]
    raw = volume.reshape(channels, planes, tiles, LANES).transpose(0, 2, 1, 3).reshape(-1, LANES)
    f32, bf16 = jnp.float32, jnp.bfloat16
    dma = pltpu.SemaphoreType.DMA
    keep = functools.partial(pltpu.with_memory_space_constraint, memory_space=pltpu.HBM)
    far = pl.BlockSpec(memory_space=pltpu.HBM)
    out = pl.pallas_call(
        functools.partial(block_body, depth, chan, groups, planes),
        in_specs=[far] * 5,
        out_specs=pl.BlockSpec(memory_space=pl.ANY),
        out_shape=jax.ShapeDtypeStruct((channels, tiles * planes, 1, LANES), f32),
        scratch_shapes=[
            pltpu.VMEM(raw.shape, f32),
            pltpu.VMEM((groups, planes, width, cells), f32),
            pltpu.VMEM((total + 2, width, cells), f32),
            pltpu.VMEM((3, (total + 2) * 9 * width, cells), bf16),
            pltpu.VMEM((3 * width, cells), f32),
            pltpu.VMEM((3, width, taps), f32),
            pltpu.VMEM((3 * width, 27 * width), f32),
            pltpu.VMEM((3, 3 * width, 27 * width), bf16),
            pltpu.VMEM((2, 2, width, cells), f32),
            pltpu.VMEM((2, 2, width, cells), f32),
            pltpu.VMEM((total, width, cells), f32),
            pltpu.VMEM((slots, every, LANES), f32),
            pltpu.VMEM((slots, every, LANES), f32),
            pltpu.VMEM((1, every), f32),
            pltpu.VMEM((hidden, every), f32),
            pltpu.VMEM((every, hidden), f32),
            pltpu.VMEM((hidden, every), bf16),
            pltpu.VMEM((hidden, every), bf16),
            pltpu.VMEM((every, hidden), bf16),
            pltpu.VMEM((every, hidden), bf16),
            pltpu.VMEM((every, 2 * LANES), bf16),
            pltpu.VMEM((every, 2 * LANES), bf16),
            pltpu.VMEM((every, 2 * LANES), f32),
            dma,
            dma((total + 2,)),
            dma((6,)),
            dma((2, groups)),
            dma((groups, planes)),
            dma((2, 2)),
            dma((2, 2)),
            dma((total, tiles)),
            dma((slots,)),
            dma((slots, chan)),
            dma,
        ],
        compiler_params=pltpu.CompilerParams(
            vmem_limit_bytes=LIMIT, collective_id=0, has_side_effects=True
        ),
        name="block",
    )(keep(raw), keep(conv_weight), keep(norm_gain), keep(mlp_in), keep(mlp_out))
    out = out.reshape(channels, tiles, planes, LANES).transpose(0, 2, 1, 3)
    return out.reshape(volume.shape)


def solution(mesh):
    in_specs = (P("chan", "depth", None), P(None, None, "chan", None, None), P(), P(), P())
    out_specs = P("chan", "depth", None)
    return jax.shard_map(
        per_device, mesh=mesh, in_specs=in_specs, out_specs=out_specs, check_vma=False
    )
```

```python
import functools

import jax
import jax.numpy as jnp
from jax import lax
from jax.experimental import pallas as pl
from jax.experimental.pallas import tpu as pltpu
from jax.sharding import PartitionSpec as P

W = 32
LANES = 128
LIMIT = 40 * 1024 * 1024
MESH = pl.DeviceIdType.MESH


def split(x):
    hi = x.astype(jnp.bfloat16)
    return hi, (x - hi.astype(jnp.float32)).astype(jnp.bfloat16)


def dot(a, b):
    return jnp.dot(a, b, preferred_element_type=jnp.float32)


def block_body(
    depth, chan, groups, planes, raw, wconv, norm, w_in, w_out, out,
    rows_in, vin, xs, xb, acc, wraw, wf, wmat, edge, halo, ybuf, rin, obuf,
    gain, in_f, out_f, in_hi, in_lo, out_hi, out_lo, r_hi, r_lo, mo,
    raw_sem, x_recv, w_sem, halo_send, swap_send, edge_send, edge_recv,
    y_send, y_recv, o_send, o_recv,
):
    width, cells = xs.shape[1:]
    total = groups * planes
    teams = depth // groups
    tiles = cells // LANES
    rows = chan // tiles
    slots = planes // rows
    channels = groups * width
    part = 3 * width
    span = 3 * part

    d = lax.axis_index("depth")
    c = lax.axis_index("chan")
    j = lax.rem(d, groups)
    t = lax.div(d, groups)
    tile = lax.rem(c, tiles)
    row = lax.div(c, tiles)
    flip = j > 0
    above = lax.rem(t + 1, teams)
    below = lax.rem(t + teams - 1, teams)

    def place(q):
        return jnp.where(flip, total - 1 - q, q)

    raw_load = pltpu.make_async_copy(raw, rows_in, raw_sem)
    raw_load.start()

    barrier = pltpu.get_barrier_semaphore()
    peers = 0
    for team in (above, below) if teams > 2 else (above,):
        for k in range(groups):
            pl.semaphore_signal(barrier, inc=1, device_id={"depth": team * groups + k}, device_id_type=MESH)
            peers += 1
    for g in range(groups):
        for k in range(1 if g == 0 else 0, chan):
            pl.semaphore_signal(
                barrier, inc=1,
                device_id={"depth": t * groups + lax.rem(j + g, groups), "chan": lax.rem(c + k, chan)},
                device_id_type=MESH,
            )
            peers += 1

    loads = [pltpu.make_async_copy(wconv.at[0, l, j], wraw.at[l], w_sem.at[l]) for l in range(3)]
    for load in loads:
        load.start()
    in_load = pltpu.make_async_copy(w_in.at[0], in_f, w_sem.at[3])
    out_load = pltpu.make_async_copy(w_out.at[0], out_f, w_sem.at[4])
    gain_load = pltpu.make_async_copy(norm, gain, w_sem.at[5])
    gain_load.start()
    in_load.start()
    out_load.start()

    def halo_copy(side, k):
        return pltpu.make_async_remote_copy(
            src_ref=vin.at[k, 0 if side == 0 else planes - 1],
            dst_ref=xs.at[total + 1 if side == 0 else 0],
            send_sem=halo_send.at[side, k],
            recv_sem=x_recv.at[total + 1 if side == 0 else 0],
            device_id={"depth": (below if side == 0 else above) * groups + k},
            device_id_type=MESH,
        )

    def swap_plane(k, i):
        peer = lax.rem(j + k, groups)
        return peer, jnp.where(peer == 0, i, planes - 1 - i)

    def swap_copy(k, i):
        peer, z = swap_plane(k, i)
        slot = j * planes + z + 1
        return pltpu.make_async_remote_copy(
            src_ref=vin.at[peer, z],
            dst_ref=xs.at[slot],
            send_sem=swap_send.at[k, i],
            recv_sem=x_recv.at[slot],
            device_id={"depth": t * groups + peer},
            device_id_type=MESH,
        )

    pitch = tiles * planes

    def fetch(k, z):
        for n in range(tiles):
            at = pl.ds(k * width * pitch + n * planes + z, width, stride=pitch)
            vin[k, z, :, n * LANES : (n + 1) * LANES] = rows_in[at, :]

    def halo_start(low, high):
        @pl.when(j == 0)
        def _():
            for k in low:
                halo_copy(0, k).start()

        @pl.when(j == groups - 1)
        def _():
            for k in high:
                halo_copy(1, k).start()

    def keep(z):
        slot = j * planes + z + 1
        pltpu.make_async_copy(vin.at[j, z], xs.at[slot], x_recv.at[slot]).start()

    raw_load.wait()
    if groups == 2:
        fetch(*swap_plane(1, 0))
        pl.semaphore_wait(barrier, peers)
        for i in range(planes):
            if i > 0:
                fetch(*swap_plane(1, i))
            swap_copy(1, i).start()
        halo_start([1], [0])
        for z in range(planes):
            fetch(j, z)
            keep(z)
        halo_start([0], [1])
    else:
        for k in range(groups):
            for z in range(planes):
                fetch(k, z)
        pl.semaphore_wait(barrier, peers)
        halo_start(range(groups), range(groups))
        for i in range(planes):
            for k in range(1, groups):
                swap_copy(k, i).start()
        for z in range(planes):
            keep(z)

    for l in range(3):
        loads[l].wait()
        for b in range(3):
            for e in range(3):
                for a in range(3):
                    start = ((b * 3 + e) * 3 + a) * width
                    piece = wraw[l, :, start : start + width]
                    hi = piece.astype(jnp.bfloat16).astype(jnp.float32)
                    for n, value in enumerate((hi, hi, piece - hi)):
                        col = ((a * 3 + n) * 3 + e) * width
                        wf[b * width : (b + 1) * width, col : col + width] = value
        wmat[l] = wf[...].astype(jnp.bfloat16)


    lane = lax.broadcasted_iota(jnp.int32, (width, LANES), 1)
    left = jnp.where(lane % W == 0, lane + W - 1, lane - 1)
    right = jnp.where(lane % W == W - 1, lane - W + 1, lane + 1)

    def prepare(l, slot, x):
        for n in range(tiles):
            at_n = slice(n * LANES, (n + 1) * LANES)
            piece = x[:, at_n]
            before = jnp.take_along_axis(piece, left, axis=1, mode="promise_in_bounds")
            after = jnp.take_along_axis(piece, right, axis=1, mode="promise_in_bounds")
            for e, value in enumerate((before, piece, after)):
                hi, lo = split(value)
                for m, kept in enumerate((hi, lo, hi)):
                    at = pl.multiple_of(slot * span + (m * 3 + e) * width, width)
                    xb[l, pl.ds(at, width), at_n] = kept

    def conv(l, p):
        at = pl.ds(pl.multiple_of(p * span, width), 3 * span)
        for n in range(0, cells, 256):
            acc[:, n : n + 256] = dot(wmat[l], xb[l, at, n : n + 256])
        p0, p1, p2 = (acc[b * width : (b + 1) * width, :] for b in range(3))
        return p1 + pltpu.roll(p0, W, 1) + pltpu.roll(p2, cells - W, 1)

    def arrive(q):
        slot = place(q) + 1
        pltpu.make_async_copy(xs.at[slot], xs.at[slot], x_recv.at[slot]).wait()
        prepare(0, slot, xs[slot])

    def edge_copy(l, side):
        front = jnp.where(flip, above, below)
        back = jnp.where(flip, below, above)
        return pltpu.make_async_remote_copy(
            src_ref=edge.at[l, side],
            dst_ref=halo.at[l, 1 - side],
            send_sem=edge_send.at[l, side],
            recv_sem=edge_recv.at[l, 1 - side],
            device_id={"depth": (front if side == 0 else back) * groups + j},
            device_id_type=MESH,
        )

    def send_edge(l, side, u):
        edge[l, side] = u
        edge_copy(l, side).start()

    def take_halo(l, side):
        pltpu.make_async_copy(halo.at[l, side], halo.at[l, side], edge_recv.at[l, side]).wait()
        prepare(l + 1, place(-1 if side == 0 else total) + 1, halo[l, side])

    def inner(l, q):
        p = place(q)
        u = jax.nn.gelu(conv(l, p))
        prepare(l + 1, p + 1, u)
        return u

    def y_target(p, k):
        z = lax.rem(p, planes)
        m = lax.div(p, planes)
        at = lax.rem(tile + tiles // 2 + k, tiles)
        peer = lax.rem(z, rows) * tiles + at
        own = jnp.logical_and(m == j, peer == c)
        src = ybuf.at[p, :, pl.ds(pl.multiple_of(at * LANES, LANES), LANES)]
        slot = lax.div(z, rows)
        first = pl.multiple_of((c * groups + j) * width, width)
        dst = rin.at[slot, pl.ds(first, width), :]
        copy = pltpu.make_async_remote_copy(
            src_ref=src, dst_ref=dst, send_sem=y_send.at[p, k], recv_sem=y_recv.at[slot],
            device_id={"depth": t * groups + m, "chan": peer}, device_id_type=MESH,
        )
        return own, copy, src, dst, y_recv.at[slot]

    def outer(q):
        p = place(q)
        ybuf[p] = xs[p + 1] + conv(2, p)

        def send(k, _):
            own, copy, src, dst, sem = y_target(p, k)

            @pl.when(own)
            def _():
                pltpu.make_async_copy(src, dst, sem).start()

            @pl.when(jnp.logical_not(own))
            def _():
                copy.start()

            return 0

        lax.fori_loop(0, tiles, send, 0)

    def own(q, _):
        arrive(q)
        return 0

    def first(q, _):
        inner(0, q)
        return 0

    lax.fori_loop(0, planes, own, 0)
    lax.fori_loop(1, planes - 1, first, 0)
    def wave(i, _):
        arrive(i + 1)
        u = inner(0, i)

        @pl.when(i == total - 1)
        def _():
            send_edge(0, 1, u)

        inner(1, i - 1)

        @pl.when(i >= 5)
        def _():
            outer(i - 2)

        return 0

    lax.fori_loop(planes - 1, total, wave, 0)
    arrive(-1)
    send_edge(0, 0, inner(0, 0))
    inner(1, 1)
    if total > 4:
        outer(2)
    take_halo(0, 0)
    send_edge(1, 0, inner(1, 0))
    outer(1)
    gain_load.wait()
    in_load.wait()
    out_load.wait()
    hidden = in_f.shape[0]
    step = 64

    def widen(k, _):
        at = pl.ds(pl.multiple_of(k * step, step), step)
        in_hi[at, :], in_lo[at, :] = split(in_f[at, :] * gain[...])
        return 0

    lax.fori_loop(0, hidden // step, widen, 0)

    def widen(k, _):
        at = pl.ds(pl.multiple_of(k * step, step), step)
        out_hi[at, :], out_lo[at, :] = split(out_f[at, :])
        return 0

    lax.fori_loop(0, out_f.shape[0] // step, widen, 0)

    take_halo(0, 1)
    send_edge(1, 1, inner(1, total - 1))
    outer(total - 2)
    take_halo(1, 1)
    outer(total - 1)
    take_halo(1, 0)
    outer(0)

    block = min(256, hidden)
    chunks = slots // 2

    def o_target(slot, k):
        peer = lax.rem(c + chan // 2 + k, chan)
        first = pl.multiple_of(peer * channels, channels)
        src = obuf.at[slot, pl.ds(first, channels), :]
        dst = out.at[:, tile * planes + slot * rows + row, 0, :]
        copy = pltpu.make_async_remote_copy(
            src_ref=src, dst_ref=dst, send_sem=o_send.at[slot, k], recv_sem=o_recv,
            device_id={"chan": peer}, device_id_type=MESH,
        )
        return peer == c, copy, src, dst

    def chunk(n, _):
        first = jnp.where(flip, n, chunks - 1 - n) * 2
        for s in range(2):
            pltpu.make_async_copy(rin.at[first + s], rin.at[first + s], y_recv.at[first + s]).wait()
            x = rin[first + s]
            r = x * lax.rsqrt(jnp.mean(x * x, axis=0, keepdims=True) + 1e-06)
            at = slice(s * LANES, (s + 1) * LANES)
            r_hi[:, at], r_lo[:, at] = split(r)
            mo[:, at] = x

        def mix(k, _):
            at = pl.ds(pl.multiple_of(k * block, block), block)
            h = dot(in_hi[at, :], r_hi[...]) + (dot(in_hi[at, :], r_lo[...]) + dot(in_lo[at, :], r_hi[...]))
            h_hi, h_lo = split(jax.nn.gelu(h))
            mo[...] += dot(out_hi[:, at], h_hi) + (dot(out_hi[:, at], h_lo) + dot(out_lo[:, at], h_hi))
            return 0

        lax.fori_loop(0, hidden // block, mix, 0)
        for s in range(2):
            obuf[first + s] = mo[:, s * LANES : (s + 1) * LANES]

            def send(k, _):
                own, copy, src, dst = o_target(first + s, k)

                @pl.when(own)
                def _():
                    pltpu.make_async_copy(src, dst, o_recv).start()

                @pl.when(jnp.logical_not(own))
                def _():
                    copy.start()

                return 0

            lax.fori_loop(0, chan, send, 0)
        return 0

    lax.fori_loop(0, chunks, chunk, 0)

    @pl.when(j == 0)
    def _():
        for k in range(groups):
            halo_copy(0, k).wait_send()

    @pl.when(j == groups - 1)
    def _():
        for k in range(groups):
            halo_copy(1, k).wait_send()

    for i in range(planes):
        for k in range(1, groups):
            swap_copy(k, i).wait_send()
    for l in range(2):
        for side in range(2):
            edge_copy(l, side).wait_send()

    def drain(n, _):
        own, copy, *_ = y_target(lax.div(n, tiles), lax.rem(n, tiles))

        @pl.when(jnp.logical_not(own))
        def _():
            copy.wait_send()

        return 0

    lax.fori_loop(0, total * tiles, drain, 0)

    def drain(n, _):
        own, copy, *_ = o_target(lax.div(n, chan), lax.rem(n, chan))

        @pl.when(jnp.logical_not(own))
        def _():
            copy.wait_send()

        return 0

    lax.fori_loop(0, slots * chan, drain, 0)
    pltpu.make_async_copy(out, out, o_recv).wait()


def per_device(volume, conv_weight, norm_gain, mlp_in, mlp_out):
    channels, planes, cells = volume.shape
    width, taps = conv_weight.shape[-2:]
    groups = channels // width
    depth, chan = lax.axis_size("depth"), lax.axis_size("chan")
    total = groups * planes
    tiles = cells // LANES
    slots = planes // (chan // tiles)
    hidden, every = mlp_in.shape[1:]
    raw = volume.reshape(channels, planes, tiles, LANES).transpose(0, 2, 1, 3).reshape(-1, LANES)
    f32, bf16 = jnp.float32, jnp.bfloat16
    dma = pltpu.SemaphoreType.DMA
    keep = functools.partial(pltpu.with_memory_space_constraint, memory_space=pltpu.HBM)
    far = pl.BlockSpec(memory_space=pltpu.HBM)
    out = pl.pallas_call(
        functools.partial(block_body, depth, chan, groups, planes),
        in_specs=[far] * 5,
        out_specs=pl.BlockSpec(memory_space=pl.ANY),
        out_shape=jax.ShapeDtypeStruct((channels, tiles * planes, 1, LANES), f32),
        scratch_shapes=[
            pltpu.VMEM(raw.shape, f32),
            pltpu.VMEM((groups, planes, width, cells), f32),
            pltpu.VMEM((total + 2, width, cells), f32),
            pltpu.VMEM((3, (total + 2) * 9 * width, cells), bf16),
            pltpu.VMEM((3 * width, cells), f32),
            pltpu.VMEM((3, width, taps), f32),
            pltpu.VMEM((3 * width, 27 * width), f32),
            pltpu.VMEM((3, 3 * width, 27 * width), bf16),
            pltpu.VMEM((2, 2, width, cells), f32),
            pltpu.VMEM((2, 2, width, cells), f32),
            pltpu.VMEM((total, width, cells), f32),
            pltpu.VMEM((slots, every, LANES), f32),
            pltpu.VMEM((slots, every, LANES), f32),
            pltpu.VMEM((1, every), f32),
            pltpu.VMEM((hidden, every), f32),
            pltpu.VMEM((every, hidden), f32),
            pltpu.VMEM((hidden, every), bf16),
            pltpu.VMEM((hidden, every), bf16),
            pltpu.VMEM((every, hidden), bf16),
            pltpu.VMEM((every, hidden), bf16),
            pltpu.VMEM((every, 2 * LANES), bf16),
            pltpu.VMEM((every, 2 * LANES), bf16),
            pltpu.VMEM((every, 2 * LANES), f32),
            dma,
            dma((total + 2,)),
            dma((6,)),
            dma((2, groups)),
            dma((groups, planes)),
            dma((2, 2)),
            dma((2, 2)),
            dma((total, tiles)),
            dma((slots,)),
            dma((slots, chan)),
            dma,
        ],
        compiler_params=pltpu.CompilerParams(
            vmem_limit_bytes=LIMIT, collective_id=0, has_side_effects=True
        ),
        name="block",
    )(keep(raw), keep(conv_weight), keep(norm_gain), keep(mlp_in), keep(mlp_out))
    out = out.reshape(channels, tiles, planes, LANES).transpose(0, 2, 1, 3)
    return out.reshape(volume.shape)


def solution(mesh):
    in_specs = (P("chan", "depth", None), P(None, None, "chan", None, None), P(), P(), P())
    out_specs = P("chan", "depth", None)
    return jax.shard_map(
        per_device, mesh=mesh, in_specs=in_specs, out_specs=out_specs, check_vma=False
    )
```
